32 devices in a mesh: rows: 8 (over z, y), grp: 4 (over x, core).
Axes of the slice: x: 2, y: 2, z: 4, core: 2. Of those that a mesh axis runs over, the one named last changes fastest.
Arguments:
- cholesky_vectors: bfloat16 [65536, 2048], P(('rows', 'grp'))
- integral_columns: float32 [65536, 64], P(('rows', 'grp'))
- residual_diag: float32 [65536], P(('rows', 'grp')), may hold values from 40 to 120
- slot_pair_block: int32 [512], P(('rows', 'grp')), may hold values from 0 to 511, as said below
- block_live: int32 [512], P(('rows', 'grp')), may hold values from 0 to 1, as said below
- pivots: int32 [64], replicated, may hold values from 0 to 65535, as said below
Outputs:
- new_columns: float32 [65536, 64], P(('rows', 'grp'))
- relative_diag: float32 [65536], P(('rows', 'grp'))
- peak: float32 [], replicated
The draws below stay inside these ranges and needn't reach their ends.
Inputs may be any that keep to these rules, and one draw needn't show every extreme that they name: `slot_pair_block`: each block number appears once. `block_live`: slots s * 16 to s * 16 + 15 are those of device s; each device has 1 to 12 surviving slots, and some device has exactly 12. Distinct; every pivot lies in a surviving slot; each device's slots hold at most 2 pivots, and some device holds exactly 2.
All inputs are finite; a program needn't handle non-finite values.
Results may differ from the reference program's by a relative error of at most 0.0003.
Values sent between devices are 32-bit elements; how exact they have to be, the bound alone decides.
A program may use at most 64 MiB of HBM per device.

```python
import jax
import jax.numpy as jnp
from jax import lax

BLK = 128
PIV = 64
K = 2048
SLOTS = 16
LIVE_MOST = 12
HOLDERS = 32
TOTAL_SLOTS = 512
NROWS = 65536
PIV_MOST = 2


def slot_layout(key):
    base = jax.random.fold_in(key, 7)
    random_keys = jax.random.split(base, 8)
    slot_pair_block = jax.random.permutation(random_keys[0], TOTAL_SLOTS).astype(jnp.int32)
    small_count = jax.random.randint(random_keys[1], (HOLDERS,), 1, max(2, LIVE_MOST // 3 + 1))
    heavy = jax.random.randint(random_keys[2], (HOLDERS,), 0, 4) == 0
    counts = jnp.where(heavy, LIVE_MOST, small_count)
    forced = jax.random.randint(random_keys[3], (), 0, HOLDERS)
    counts = jnp.where(jnp.arange(HOLDERS) == forced, LIVE_MOST, counts)
    scores = jax.random.randint(random_keys[4], (HOLDERS, SLOTS), 0, 1000) * SLOTS + jnp.arange(SLOTS)[None, :]
    ranks = jnp.argsort(jnp.argsort(scores, axis=1), axis=1)
    live = (ranks < counts[:, None]).astype(jnp.int32)
    holder_order = jax.random.permutation(random_keys[5], HOLDERS)
    index = jnp.arange(PIV)
    holder = holder_order[index % HOLDERS]
    within = index // HOLDERS
    choose = live[holder] * (SLOTS * 1000) + jax.random.randint(random_keys[6], (PIV, SLOTS), 0, 1000) * SLOTS + jnp.arange(SLOTS)[None, :]
    slot = jnp.argmax(choose, axis=1)
    offset = jax.random.randint(random_keys[7], (PIV,), 0, BLK // PIV_MOST) * PIV_MOST + within
    global_slot = holder * SLOTS + slot
    pivot_ids = (slot_pair_block[global_slot] * BLK + offset).astype(jnp.int32)
    pivot_rows = (global_slot * BLK + offset).astype(jnp.int32)
    return (slot_pair_block, live.reshape(-1), pivot_ids, pivot_rows)


def draw_slot_pair_block(key, part):
    return slot_layout(key)[0]


def draw_block_live(key, part):
    return slot_layout(key)[1]


def draw_pivots(key, part):
    return slot_layout(key)[2]


def draw_cholesky_vectors(key, part):
    inner = jax.random.fold_in(key, 31)
    spread = K ** (-0.25)
    values = jax.random.normal(inner, (NROWS, K), jnp.float32)
    return (values * spread).astype(jnp.bfloat16)


def draw_integral_columns(key, part):
    vectors = draw_cholesky_vectors(key, part)
    pivot_rows = slot_layout(key)[3]
    picked = vectors[pivot_rows]
    gram = jnp.dot(picked, picked.T, preferred_element_type=jnp.float32)
    random_keys = jax.random.split(jax.random.fold_in(key, 53), 3)
    diag_part = jax.random.uniform(random_keys[0], (PIV,), jnp.float32, 14.0, 40.0)
    coupling = jax.random.uniform(random_keys[1], (PIV, PIV), jnp.float32, -0.4, 0.4)
    coupling = (coupling + coupling.T) * 0.5 * (1.0 - jnp.eye(PIV, dtype=jnp.float32))
    block = gram + jnp.diag(diag_part) + coupling
    filler = jax.random.normal(random_keys[2], (NROWS, PIV), jnp.float32)
    return filler.at[pivot_rows].set(block)


def levels(stream_key, dims, cuts, least, top_value):
    factor_of, own = 1.0, jax.random.fold_in(stream_key, 6)
    for axis_at, shards_of in cuts:
        steps = jnp.exp(jax.random.uniform(jax.random.fold_in(own, axis_at), (shards_of,), jnp.float32, least / len(cuts), top_value / len(cuts)))
        factor_of = factor_of * jnp.repeat(steps, dims[axis_at] // shards_of).reshape([-1 if axis == axis_at else 1 for axis in range(len(dims))])
    return factor_of


def setup_inputs(seed: int = 0) -> dict:
    seeds = jax.random.split(jax.random.key(seed), 7)
    cholesky_vectors = draw_cholesky_vectors(jax.random.fold_in(seeds[6], 71), 0)
    integral_columns = draw_integral_columns(jax.random.fold_in(seeds[6], 71), 0)
    residual_diag = jnp.clip(40.0 + 80.0 * jax.random.uniform(seeds[2], (NROWS,), jnp.float32) ** levels(seeds[2], (NROWS,), ((0, 32),), -0.2, 0.2), 40.0, 120.0)
    slot_pair_block = draw_slot_pair_block(jax.random.fold_in(seeds[6], 71), 0)
    block_live = draw_block_live(jax.random.fold_in(seeds[6], 71), 0)
    pivots = draw_pivots(jax.random.fold_in(seeds[6], 71), 0)
    return dict(cholesky_vectors=cholesky_vectors, integral_columns=integral_columns, residual_diag=residual_diag, slot_pair_block=slot_pair_block, block_live=block_live, pivots=pivots)


def reference(cholesky_vectors, integral_columns, residual_diag, slot_pair_block, block_live, pivots):
    block_slot_lookup = jnp.zeros((TOTAL_SLOTS,), jnp.int32).at[slot_pair_block].set(jnp.arange(TOTAL_SLOTS, dtype=jnp.int32))
    pivot_rows = (block_slot_lookup[pivots // BLK] * BLK + pivots % BLK).astype(jnp.int32)
    picked = cholesky_vectors[pivot_rows]
    pivot_block = integral_columns[pivot_rows]
    gram = jnp.dot(picked.astype(jnp.float32), picked.T.astype(jnp.float32), preferred_element_type=jnp.float32)
    lower_factor = jnp.linalg.cholesky(pivot_block - gram)
    remain = integral_columns - jnp.dot(cholesky_vectors.astype(jnp.float32), picked.T.astype(jnp.float32), preferred_element_type=jnp.float32)
    columns = lax.linalg.triangular_solve(lower_factor, remain, left_side=False, lower=True, transpose_a=True)
    live_rows = jnp.repeat(block_live, BLK) > 0
    columns = jnp.where(live_rows[:, None], columns, 0.0)
    updated = jnp.where(live_rows, residual_diag - jnp.sum(columns * columns, axis=1), residual_diag)
    is_pivot = jnp.zeros((NROWS,), jnp.int32).at[pivot_rows].set(1) > 0
    updated = jnp.where(is_pivot, 0.0, updated)
    peak = jnp.max(jnp.where(live_rows, updated, 0.0))
    return (columns, updated / peak, peak)
```

```python
import functools

import jax
import jax.numpy as jnp
from jax import lax
from jax.experimental import pallas as pl
from jax.experimental.pallas import tpu as pltpu
from jax.sharding import PartitionSpec as P

MESH = pl.DeviceIdType.MESH
LANES = 128


def step_kernel(
    sizes, vec_hbm, col_hbm, res_ref, slot_ref, live_ref, piv_ref,
    new_hbm, rel_ref, peak_ref,
    vec, col, new, send, got, mine, tops, sums, marks,
    vec_sem, col_sem, own_sem, send_sem, chip_sem, core_sem, top_send, top_recv, out_sem,
):
    n_rows, n_grp, per, block, rows_sent, part = sizes
    n = n_rows * n_grp
    total, depth = vec.shape
    slots = total // block
    piv = col.shape[0]
    chunks = depth // LANES
    parts = total // part
    my_row, my_grp = lax.axis_index("rows"), lax.axis_index("grp")
    me = my_row * n_grp + my_grp
    side = lax.rem(my_grp, 2)
    partner_grp = my_grp + 1 - 2 * side
    half = n // 2
    my_chip = me // 2
    over_first = (((0,), (0,)), ((), ()))
    over_last = (((1,), (1,)), ((), ()))

    def place(flat):
        return (flat // n_grp, lax.rem(flat, n_grp))

    def dot_t(a, b):
        return lax.dot_general(a, b, over_last, preferred_element_type=jnp.float32)

    def split(x):
        hi = x.astype(jnp.bfloat16)
        return hi, x - hi.astype(jnp.float32)

    col_copy = pltpu.make_async_copy(col_hbm, col, col_sem)
    col_copy.start()
    vec_copies = [
        pltpu.make_async_copy(
            vec_hbm.at[pl.ds(i * part, part), :], vec.at[pl.ds(i * part, part), :], vec_sem.at[i]
        )
        for i in range(parts)
    ]
    for copy in vec_copies:
        copy.start()

    barrier = pltpu.get_barrier_semaphore()

    def greet(t, carry):
        pl.semaphore_signal(
            barrier, inc=1, device_id=place(lax.rem(me + t, n)), device_id_type=MESH
        )
        return carry

    lax.fori_loop(1, n, greet, 0)

    def iota(shape, axis):
        return lax.broadcasted_iota(jnp.int32, shape, axis)

    def upright(row, size):
        return jnp.sum(
            jnp.where(iota((size, size), 0) == iota((size, size), 1), row, 0), axis=1, keepdims=True
        )

    piv_row = piv_ref[...]
    slot_row = slot_ref[...]
    piv_col = upright(piv_row, piv)
    slot_col = upright(slot_row, slots)
    live_col = upright(live_ref[...], slots)
    group_col, offset_col = piv_col // block, lax.rem(piv_col, block)
    match = jnp.where(group_col == slot_row, 1, 0)
    owned_col = jnp.max(match, axis=1, keepdims=True)
    owned_row = jnp.max(jnp.where(slot_col == piv_row // block, 1, 0), axis=0, keepdims=True)
    before = jnp.where(iota((piv, piv), 0) < iota((piv, piv), 1), owned_col, 0)
    rank_row = jnp.sum(before, axis=0, keepdims=True)
    selector = jnp.where((rank_row == iota((8, piv), 0)) & (owned_row > 0), 1.0, 0.0)
    ids = (
        jnp.sum(selector * (iota((8, piv), 1) + 1).astype(jnp.float32), axis=1, keepdims=True) - 1.0
    )
    selector = selector.astype(jnp.bfloat16)
    hot = []
    here = offset_col == iota((piv, block), 1)
    for s in range(slots):
        at_s = jnp.where(here, match[:, s : s + 1], 0).astype(jnp.float32)
        marks[s : s + 1, :] = jnp.max(at_s, axis=0, keepdims=True)
        hot.append(jnp.dot(selector, at_s.astype(jnp.bfloat16), preferred_element_type=jnp.float32))
    hot = jnp.concatenate(hot, axis=1).astype(jnp.bfloat16)

    send[...] = jnp.zeros_like(send)
    own = jnp.zeros((8, depth), jnp.float32)
    for i in range(parts):
        vec_copies[i].wait()
        at = slice(i * part, (i + 1) * part)
        own = own + jnp.dot(hot[:, at], vec[at, :], preferred_element_type=jnp.float32)
    col_copy.wait()
    col_hi, rest = split(col[...])
    col_mid, rest = split(rest)
    own_col = dot_t(hot, col_hi) + (dot_t(hot, col_mid) + dot_t(hot, rest.astype(jnp.bfloat16)))
    aside = jnp.concatenate([own_col, jnp.broadcast_to(ids, (8, piv))], axis=1)
    for j in range(per):
        for c in range(chunks):
            send[j * chunks + c : j * chunks + c + 1, :] = own[
                j : j + 1, c * LANES : (c + 1) * LANES
            ]
        send[per * chunks + j : per * chunks + j + 1, 0 : 2 * piv] = aside[j : j + 1, :]

    pl.semaphore_wait(barrier, n - 1)

    def slot_of(flat):
        return got.at[pl.ds(pl.multiple_of(flat * rows_sent, 8), rows_sent), :]

    own_copy = pltpu.make_async_copy(send, slot_of(me), own_sem)
    own_copy.start()

    def to_chip(chip):
        flat = chip * 2 + side
        return pltpu.make_async_remote_copy(
            src_ref=send, dst_ref=slot_of(me), send_sem=send_sem, recv_sem=chip_sem.at[my_chip],
            device_id=place(flat), device_id_type=MESH,
        )

    def send_chip(t, carry):
        to_chip(lax.rem(my_chip + t, half)).start()
        return carry

    lax.fori_loop(1, half, send_chip, 0)
    pltpu.make_async_remote_copy(
        src_ref=send, dst_ref=slot_of(me), send_sem=send_sem, recv_sem=core_sem,
        device_id=(my_row, partner_grp), device_id_type=MESH,
    ).start()

    def relay(t, carry):
        chip = lax.rem(my_chip + half - t, half)
        flat = chip * 2 + side
        pltpu.make_async_remote_copy(
            src_ref=send, dst_ref=slot_of(flat), send_sem=send_sem, recv_sem=chip_sem.at[chip],
            device_id=(my_row, partner_grp), device_id_type=MESH,
        ).wait_recv()
        pltpu.make_async_remote_copy(
            src_ref=slot_of(flat), dst_ref=slot_of(flat), send_sem=send_sem, recv_sem=core_sem,
            device_id=(my_row, partner_grp), device_id_type=MESH,
        ).start()
        return carry

    lax.fori_loop(1, half, relay, 0)
    half_ref = got.at[pl.ds(0, half * rows_sent), :]
    own_copy.wait()
    pltpu.make_async_remote_copy(
        src_ref=half_ref, dst_ref=half_ref, send_sem=send_sem, recv_sem=core_sem,
        device_id=(my_row, partner_grp), device_id_type=MESH,
    ).wait_recv()

    arrived = jnp.concatenate(
        [
            jnp.concatenate(
                [
                    got[pl.ds(j * chunks + c, n, stride=rows_sent), :].astype(jnp.bfloat16)
                    for c in range(chunks)
                ],
                axis=1,
            )
            for j in range(per)
        ],
        axis=0,
    )
    aside = jnp.concatenate(
        [got[pl.ds(per * chunks + j, n, stride=rows_sent), :] for j in range(per)], axis=0
    )
    order = lax.broadcasted_iota(jnp.int32, (n * per, piv), 1).astype(jnp.float32)
    placing = jnp.where(aside[:, piv : 2 * piv] == order, 1.0, 0.0)
    picked = lax.dot_general(
        placing.astype(jnp.bfloat16), arrived, over_first, preferred_element_type=jnp.float32
    ).astype(jnp.bfloat16)
    pivot_block = lax.dot_general(
        placing, aside[:, 0:piv], over_first, precision=lax.Precision.HIGHEST,
        preferred_element_type=jnp.float32,
    )
    gram = lax.dot_general(picked, picked, over_last, preferred_element_type=jnp.float32)
    sub = lax.broadcasted_iota(jnp.int32, (piv, piv), 0)
    lan = lax.broadcasted_iota(jnp.int32, (piv, piv), 1)
    eye = jnp.where(sub == lan, 1.0, 0.0)
    state = jnp.concatenate([pivot_block - gram, eye], axis=1)
    sub_col = lax.broadcasted_iota(jnp.int32, (piv, 1), 0)
    every = max(1, piv // parts)
    done = 0

    def subtract(i):
        at = slice(i * part, (i + 1) * part)
        new[:, at] = col[:, at] - dot_t(picked, vec[at, :])

    for k in range(piv):
        scale = 1.0 / state[k : k + 1, k : k + 1]
        mult = jnp.where(sub_col > k, state[:, k : k + 1] * scale, 0.0)
        state = state - mult * state[k : k + 1, :]
        if k % every == every - 1 and done < parts:
            subtract(done)
            done += 1
    for i in range(done, parts):
        subtract(i)
    diag = jnp.sum(jnp.where(sub == lan, state[:, 0:piv], 0.0), axis=1, keepdims=True)
    inverse = state[:, piv : 2 * piv] * lax.rsqrt(diag)
    inv_hi, rest = split(inverse)
    inv_lo = rest.astype(jnp.bfloat16)
    wide = jnp.concatenate([inv_hi, inv_lo, inv_hi, inv_lo], axis=1)
    for i in range(parts):
        at = slice(i * part, (i + 1) * part)
        rem_hi, rest = split(new[:, at])
        rem_lo = rest.astype(jnp.bfloat16)
        tall = jnp.concatenate([rem_hi, rem_hi, rem_lo, rem_lo], axis=0)
        value = jnp.dot(wide, tall, preferred_element_type=jnp.float32)
        for s in range(i * part // block, (i + 1) * part // block):
            lane = slice(s * block - i * part, (s + 1) * block - i * part)
            kept = jnp.where(live_col[s : s + 1, :] > 0, value[:, lane], 0.0)
            new[:, s * block : (s + 1) * block] = kept
            sums[s : s + 1, :] = jnp.sum(kept * kept, axis=0, keepdims=True)
    out_copy = pltpu.make_async_copy(new, new_hbm, out_sem)
    out_copy.start()

    alive = jnp.broadcast_to(live_col, (slots, block)) > 0
    updated = res_ref[...] - jnp.where(alive, sums[...], 0.0)
    updated = jnp.where(marks[...] > 0.0, 0.0, updated)
    best = jnp.max(jnp.where(alive, updated, 0.0), axis=(0, 1), keepdims=True)
    mine[...] = jnp.broadcast_to(best, mine.shape)

    def tell(t, carry):
        pltpu.make_async_remote_copy(
            src_ref=mine, dst_ref=tops.at[me], send_sem=top_send, recv_sem=top_recv,
            device_id=place(lax.rem(me + t, n)), device_id_type=MESH,
        ).start()
        return carry

    lax.fori_loop(1, n, tell, 0)
    top_own = pltpu.make_async_copy(mine, tops.at[me], own_sem)
    top_own.start()
    top_own.wait()
    others = pltpu.make_async_remote_copy(
        src_ref=tops.at[pl.ds(0, n - 1)], dst_ref=tops.at[pl.ds(0, n - 1)],
        send_sem=top_send, recv_sem=top_recv,
        device_id=(my_row, partner_grp), device_id_type=MESH,
    )
    others.wait_recv()
    peak = jnp.max(jnp.max(tops[...], axis=0), axis=1, keepdims=True)
    peak_ref[...] = peak
    rel_ref[...] = updated / peak
    others.wait_send()
    pltpu.make_async_remote_copy(
        src_ref=half_ref, dst_ref=half_ref, send_sem=send_sem, recv_sem=core_sem,
        device_id=(my_row, partner_grp), device_id_type=MESH,
    ).wait_send()
    rest_ref = got.at[pl.ds(0, (half - 1) * rows_sent), :]
    pltpu.make_async_remote_copy(
        src_ref=rest_ref, dst_ref=rest_ref, send_sem=send_sem, recv_sem=core_sem,
        device_id=(my_row, partner_grp), device_id_type=MESH,
    ).wait_send()
    out_copy.wait()


def solution(mesh):
    n_rows, n_grp = mesh.shape["rows"], mesh.shape["grp"]
    n = n_rows * n_grp

    def on_device(vectors, columns, residual, slot_block, live, pivots):
        total, depth = vectors.shape
        slots = slot_block.shape[0]
        block = total // slots
        piv = pivots.shape[0]
        per = max(1, piv // n)
        chunks = depth // LANES
        part = 2 * block if slots % 2 == 0 else block
        rows_sent = -(-(per * (chunks + 1)) // 8) * 8
        hbm = pl.BlockSpec(memory_space=pl.ANY)
        vmem = pl.BlockSpec(memory_space=pltpu.VMEM)
        smem = pl.BlockSpec(memory_space=pltpu.SMEM)
        dma = pltpu.SemaphoreType.DMA
        new, rel, peak = pl.pallas_call(
            functools.partial(step_kernel, (n_rows, n_grp, per, block, rows_sent, part)),
            out_shape=(
                jax.ShapeDtypeStruct((piv, total), jnp.float32),
                jax.ShapeDtypeStruct((slots, block), jnp.float32),
                jax.ShapeDtypeStruct((1, 1), jnp.float32),
            ),
            in_specs=[hbm, hbm, vmem, vmem, vmem, vmem],
            out_specs=(hbm, vmem, vmem),
            scratch_shapes=[
                pltpu.VMEM((total, depth), jnp.bfloat16),
                pltpu.VMEM((piv, total), jnp.float32),
                pltpu.VMEM((piv, total), jnp.float32),
                pltpu.VMEM((rows_sent, LANES), jnp.float32),
                pltpu.VMEM((n * rows_sent, LANES), jnp.float32),
                pltpu.VMEM((1, LANES), jnp.float32),
                pltpu.VMEM((n, 1, LANES), jnp.float32),
                pltpu.VMEM((slots, block), jnp.float32),
                pltpu.VMEM((slots, block), jnp.float32),
                dma((total // part,)), dma, dma, dma, dma((n // 2,)), dma, dma, dma, dma,
            ],
            compiler_params=pltpu.CompilerParams(
                collective_id=0, has_side_effects=True, vmem_limit_bytes=48 << 20
            ),
        )(
            vectors, columns.T, residual.reshape(slots, block), slot_block.reshape(1, slots),
            live.reshape(1, slots), pivots.reshape(1, piv),
        )
        return new.T, rel.reshape(total), peak.reshape(())

    spread = P(("rows", "grp"))
    return jax.shard_map(
        on_device,
        mesh=mesh,
        in_specs=(P(("rows", "grp"), None), P(("rows", "grp"), None), spread, spread, spread, P()),
        out_specs=(P(("rows", "grp"), None), spread, P()),
        check_vma=False,
    )
```

```python
import functools

import jax
import jax.numpy as jnp
from jax import lax
from jax.experimental import pallas as pl
from jax.experimental.pallas import tpu as pltpu
from jax.sharding import PartitionSpec as P

MESH = pl.DeviceIdType.MESH
LANES = 128


def step_kernel(
    sizes, vec_hbm, col_hbm, res_hbm, slot_hbm, live_hbm, piv_hbm,
    new_hbm, rel_hbm, peak_hbm,
    vec, col, res_ref, slot_ref, live_ref, piv_ref, new, rel_ref, peak_ref, send, got, mine, tops, sums, marks,
    small_sem, vec_sem, col_sem, own_sem, send_sem, chip_sem, core_sem, top_send, top_recv, out_sem,
):
    n_rows, n_grp, per, block, rows_sent, part = sizes
    n = n_rows * n_grp
    total, depth = vec.shape
    slots = total // block
    piv = col.shape[0]
    chunks = depth // LANES
    parts = total // part
    used = per * (chunks + 1)
    my_row, my_grp = lax.axis_index("rows"), lax.axis_index("grp")
    me = my_row * n_grp + my_grp
    side = lax.rem(my_grp, 2)
    partner_grp = my_grp + 1 - 2 * side
    half = n // 2
    my_chip = me // 2
    over_first = (((0,), (0,)), ((), ()))
    over_last = (((1,), (1,)), ((), ()))

    def place(flat):
        return (flat // n_grp, lax.rem(flat, n_grp))

    def dot_t(a, b):
        return lax.dot_general(a, b, over_last, preferred_element_type=jnp.float32)

    def split(x):
        hi = x.astype(jnp.bfloat16)
        return hi, x - hi.astype(jnp.float32)

    small_copies = [
        pltpu.make_async_copy(source, target, small_sem.at[i])
        for i, (source, target) in enumerate(
            ((piv_hbm, piv_ref), (slot_hbm, slot_ref), (live_hbm, live_ref), (res_hbm, res_ref))
        )
    ]
    for copy in small_copies:
        copy.start()
    col_copy = pltpu.make_async_copy(col_hbm, col, col_sem)
    vec_copies = [
        pltpu.make_async_copy(
            vec_hbm.at[pl.ds(i * part, part), :], vec.at[pl.ds(i * part, part), :], vec_sem.at[i]
        )
        for i in range(parts)
    ]
    for copy in vec_copies:
        copy.start()
    col_copy.start()

    barrier = pltpu.get_barrier_semaphore()

    def greet(t, carry):
        pl.semaphore_signal(
            barrier, inc=1, device_id=place(lax.rem(me + t, n)), device_id_type=MESH
        )
        return carry

    lax.fori_loop(1, n, greet, 0)

    def iota(shape, axis):
        return lax.broadcasted_iota(jnp.int32, shape, axis)

    def upright(row, size):
        return jnp.sum(
            jnp.where(iota((size, size), 0) == iota((size, size), 1), row, 0), axis=1, keepdims=True
        )

    for copy in small_copies:
        copy.wait()
    piv_row = piv_ref[...]
    slot_row = slot_ref[...]
    piv_col = upright(piv_row, piv)
    slot_col = upright(slot_row, slots)
    live_col = upright(live_ref[...], slots)
    group_col, offset_col = piv_col // block, lax.rem(piv_col, block)
    match = jnp.where(group_col == slot_row, 1, 0)
    owned_col = jnp.max(match, axis=1, keepdims=True)
    owned_row = jnp.max(jnp.where(slot_col == piv_row // block, 1, 0), axis=0, keepdims=True)
    before = jnp.where(iota((piv, piv), 0) < iota((piv, piv), 1), owned_col, 0)
    rank_row = jnp.sum(before, axis=0, keepdims=True)
    selector = jnp.where((rank_row == iota((8, piv), 0)) & (owned_row > 0), 1.0, 0.0)
    ids = (
        jnp.sum(selector * (iota((8, piv), 1) + 1).astype(jnp.float32), axis=1, keepdims=True) - 1.0
    )
    selector = selector.astype(jnp.bfloat16)
    hot = []
    here = offset_col == iota((piv, block), 1)
    for s in range(slots):
        at_s = jnp.where(here, match[:, s : s + 1], 0).astype(jnp.float32)
        marks[s : s + 1, :] = jnp.max(at_s, axis=0, keepdims=True)
        hot.append(jnp.dot(selector, at_s.astype(jnp.bfloat16), preferred_element_type=jnp.float32))
    hot = jnp.concatenate(hot, axis=1).astype(jnp.bfloat16)

    send[...] = jnp.zeros_like(send)
    own = jnp.zeros((8, depth), jnp.float32)
    for i in range(parts):
        vec_copies[i].wait()
        at = slice(i * part, (i + 1) * part)
        own = own + jnp.dot(hot[:, at], vec[at, :], preferred_element_type=jnp.float32)
    col_copy.wait()
    col_hi, rest = split(col[...])
    col_mid, rest = split(rest)
    own_col = dot_t(hot, col_hi) + (dot_t(hot, col_mid) + dot_t(hot, rest.astype(jnp.bfloat16)))
    aside = jnp.concatenate([own_col, jnp.broadcast_to(ids, (8, piv))], axis=1)
    for j in range(per):
        for c in range(chunks):
            send[j * chunks + c : j * chunks + c + 1, :] = own[
                j : j + 1, c * LANES : (c + 1) * LANES
            ]
        send[per * chunks + j : per * chunks + j + 1, 0 : 2 * piv] = aside[j : j + 1, :]

    pl.semaphore_wait(barrier, n - 1)

    def slot_of(flat):
        return got.at[pl.ds(pl.multiple_of(flat * rows_sent, 8), used), :]

    own_copy = pltpu.make_async_copy(send.at[pl.ds(0, used), :], slot_of(me), own_sem)
    own_copy.start()

    def to_chip(chip):
        flat = chip * 2 + side
        return pltpu.make_async_remote_copy(
            src_ref=send.at[pl.ds(0, used), :], dst_ref=slot_of(me), send_sem=send_sem, recv_sem=chip_sem.at[my_chip],
            device_id=place(flat), device_id_type=MESH,
        )

    def send_chip(t, carry):
        to_chip(lax.rem(my_chip + t, half)).start()
        return carry

    lax.fori_loop(1, half, send_chip, 0)
    pltpu.make_async_remote_copy(
        src_ref=send.at[pl.ds(0, used), :], dst_ref=slot_of(me), send_sem=send_sem, recv_sem=core_sem,
        device_id=(my_row, partner_grp), device_id_type=MESH,
    ).start()

    def relay(t, carry):
        chip = lax.rem(my_chip + half - t, half)
        flat = chip * 2 + side
        pltpu.make_async_remote_copy(
            src_ref=send.at[pl.ds(0, used), :], dst_ref=slot_of(flat), send_sem=send_sem, recv_sem=chip_sem.at[chip],
            device_id=(my_row, partner_grp), device_id_type=MESH,
        ).wait_recv()
        pltpu.make_async_remote_copy(
            src_ref=slot_of(flat), dst_ref=slot_of(flat), send_sem=send_sem, recv_sem=core_sem,
            device_id=(my_row, partner_grp), device_id_type=MESH,
        ).start()
        return carry

    lax.fori_loop(1, half, relay, 0)
    half_ref = got.at[pl.ds(0, half * used), :]
    own_copy.wait()
    pltpu.make_async_remote_copy(
        src_ref=half_ref, dst_ref=half_ref, send_sem=send_sem, recv_sem=core_sem,
        device_id=(my_row, partner_grp), device_id_type=MESH,
    ).wait_recv()

    arrived = jnp.concatenate(
        [
            jnp.concatenate(
                [
                    got[pl.ds(j * chunks + c, n, stride=rows_sent), :].astype(jnp.bfloat16)
                    for c in range(chunks)
                ],
                axis=1,
            )
            for j in range(per)
        ],
        axis=0,
    )
    aside = jnp.concatenate(
        [got[pl.ds(per * chunks + j, n, stride=rows_sent), :] for j in range(per)], axis=0
    )
    order = lax.broadcasted_iota(jnp.int32, (n * per, piv), 1).astype(jnp.float32)
    placing = jnp.where(aside[:, piv : 2 * piv] == order, 1.0, 0.0)
    picked = lax.dot_general(
        placing.astype(jnp.bfloat16), arrived, over_first, preferred_element_type=jnp.float32
    ).astype(jnp.bfloat16)
    pivot_block = lax.dot_general(
        placing, aside[:, 0:piv], over_first, precision=lax.Precision.HIGHEST,
        preferred_element_type=jnp.float32,
    )
    gram = lax.dot_general(picked, picked, over_last, preferred_element_type=jnp.float32)
    sub, lan = iota((piv, piv), 0), iota((piv, piv), 1)
    eye = jnp.where(sub == lan, 1.0, 0.0)
    state = jnp.concatenate([pivot_block - gram, eye], axis=1)
    tile = 8
    bands = [state[t : t + tile, :] for t in range(0, piv, tile)]
    sub_col = iota((tile, 1), 0)
    every = max(1, piv // parts)
    done = 0

    def subtract(i):
        at = slice(i * part, (i + 1) * part)
        new[:, at] = col[:, at] - dot_t(picked, vec[at, :])

    state = jnp.concatenate(bands, axis=0)
    wide_col = iota((piv, 1), 0)
    for k in range(piv):
        scale = 1.0 / state[k : k + 1, k : k + 1]
        mult = jnp.where(wide_col > k, state[:, k : k + 1] * scale, 0.0)
        state = state - mult * state[k : k + 1, :]
        if k % every == every - 1 and done < parts:
            subtract(done)
            done += 1
    for i in range(done, parts):
        subtract(i)
    diag = jnp.sum(jnp.where(sub == lan, state[:, 0:piv], 0.0), axis=1, keepdims=True)
    inverse = state[:, piv : 2 * piv] * lax.rsqrt(diag)
    inv_hi, rest = split(inverse)
    inv_lo = rest.astype(jnp.bfloat16)
    wide = jnp.concatenate([inv_hi, inv_lo, inv_hi, inv_lo], axis=1)
    for i in range(parts):
        at = slice(i * part, (i + 1) * part)
        rem_hi, rest = split(new[:, at])
        rem_lo = rest.astype(jnp.bfloat16)
        tall = jnp.concatenate([rem_hi, rem_hi, rem_lo, rem_lo], axis=0)
        value = jnp.dot(wide, tall, preferred_element_type=jnp.float32)
        for s in range(i * part // block, (i + 1) * part // block):
            lane = slice(s * block - i * part, (s + 1) * block - i * part)
            kept = jnp.where(live_col[s : s + 1, :] > 0, value[:, lane], 0.0)
            new[:, s * block : (s + 1) * block] = kept
            sums[s : s + 1, :] = jnp.sum(kept * kept, axis=0, keepdims=True)

    out_copies = [
        pltpu.make_async_copy(source, target, out_sem.at[i])
        for i, (source, target) in enumerate(
            ((new, new_hbm), (rel_ref, rel_hbm), (peak_ref, peak_hbm))
        )
    ]
    out_copies[0].start()

    alive = jnp.broadcast_to(live_col, (slots, block)) > 0
    updated = res_ref[...] - jnp.where(alive, sums[...], 0.0)
    updated = jnp.where(marks[...] > 0.0, 0.0, updated)
    best = jnp.max(jnp.where(alive, updated, 0.0), axis=(0, 1), keepdims=True)
    mine[...] = jnp.broadcast_to(best, mine.shape)

    def tell(t, carry):
        pltpu.make_async_remote_copy(
            src_ref=mine, dst_ref=tops.at[me], send_sem=top_send, recv_sem=top_recv,
            device_id=place(lax.rem(me + t, n)), device_id_type=MESH,
        ).start()
        return carry

    lax.fori_loop(1, n, tell, 0)
    top_own = pltpu.make_async_copy(mine, tops.at[me], own_sem)
    top_own.start()
    top_own.wait()
    others = pltpu.make_async_remote_copy(
        src_ref=tops.at[pl.ds(0, n - 1)], dst_ref=tops.at[pl.ds(0, n - 1)],
        send_sem=top_send, recv_sem=top_recv,
        device_id=(my_row, partner_grp), device_id_type=MESH,
    )
    others.wait_recv()
    peak = jnp.max(jnp.max(tops[...], axis=0), axis=1, keepdims=True)
    peak_ref[...] = peak
    rel_ref[...] = updated / peak
    out_copies[1].start()
    out_copies[2].start()
    others.wait_send()
    pltpu.make_async_remote_copy(
        src_ref=half_ref, dst_ref=half_ref, send_sem=send_sem, recv_sem=core_sem,
        device_id=(my_row, partner_grp), device_id_type=MESH,
    ).wait_send()
    rest_ref = got.at[pl.ds(0, (half - 1) * used), :]
    pltpu.make_async_remote_copy(
        src_ref=rest_ref, dst_ref=rest_ref, send_sem=send_sem, recv_sem=core_sem,
        device_id=(my_row, partner_grp), device_id_type=MESH,
    ).wait_send()
    for copy in out_copies:
        copy.wait()


def finish_kernel(pieces, *refs):
    sources, targets, buffers, (in_sem, out_sem) = refs[0:3], refs[3:6], refs[6:9], refs[9:11]
    width = sources[0].shape[1] // pieces
    moves = [(1, slice(None)), (2, slice(None))]
    moves += [(0, slice(p * width, (p + 1) * width)) for p in range(pieces)]
    ins, outs = [], []
    for i, (which, at) in enumerate(moves):
        source, buffer, target = (
            side[which].at[:, at] for side in (sources, buffers, targets)
        )
        ins.append(pltpu.make_async_copy(source, buffer, in_sem.at[i]))
        outs.append(pltpu.make_async_copy(buffer, target, out_sem.at[i]))
    for copy in ins:
        copy.start()
    for arriving, leaving in zip(ins, outs):
        arriving.wait()
        leaving.start()
    for copy in outs:
        copy.wait()


def solution(mesh):
    n_rows, n_grp = mesh.shape["rows"], mesh.shape["grp"]
    n = n_rows * n_grp

    def on_device(vectors, columns, residual, slot_block, live, pivots):
        total, depth = vectors.shape
        slots = slot_block.shape[0]
        block = total // slots
        piv = pivots.shape[0]
        per = max(1, piv // n)
        chunks = depth // LANES
        part = 2 * block if slots % 2 == 0 else block
        rows_sent = -(-(per * (chunks + 1)) // 8) * 8
        hbm = pl.BlockSpec(memory_space=pltpu.HBM)
        dma = pltpu.SemaphoreType.DMA
        shapes = (
            jax.ShapeDtypeStruct((piv, total), jnp.float32),
            jax.ShapeDtypeStruct((slots, block), jnp.float32),
            jax.ShapeDtypeStruct((1, 1), jnp.float32),
        )
        new, rel, peak = pl.pallas_call(
            functools.partial(step_kernel, (n_rows, n_grp, per, block, rows_sent, part)),
            out_shape=shapes,
            in_specs=[hbm] * 6,
            out_specs=(hbm,) * 3,
            scratch_shapes=[
                pltpu.VMEM((total, depth), jnp.bfloat16),
                pltpu.VMEM((piv, total), jnp.float32),
                pltpu.VMEM((slots, block), jnp.float32),
                pltpu.VMEM((1, slots), jnp.int32),
                pltpu.VMEM((1, slots), jnp.int32),
                pltpu.VMEM((1, piv), jnp.int32),
                *(pltpu.VMEM(shape.shape, shape.dtype) for shape in shapes),
                pltpu.VMEM((rows_sent, LANES), jnp.float32),
                pltpu.VMEM((n * rows_sent, LANES), jnp.float32),
                pltpu.VMEM((1, LANES), jnp.float32),
                pltpu.VMEM((n, 1, LANES), jnp.float32),
                pltpu.VMEM((slots, block), jnp.float32),
                pltpu.VMEM((slots, block), jnp.float32),
                dma((4,)), dma((total // part,)), dma, dma, dma, dma((n // 2,)), dma, dma, dma, dma((3,)),
            ],
            compiler_params=pltpu.CompilerParams(
                collective_id=0, has_side_effects=True, vmem_limit_bytes=62 << 20
            ),
        )(
            vectors, columns.T, residual.reshape(slots, block), slot_block.reshape(1, slots),
            live.reshape(1, slots), pivots.reshape(1, piv),
        )
        pieces = 4
        new, rel, peak = pl.pallas_call(
            functools.partial(finish_kernel, pieces),
            out_shape=shapes,
            in_specs=[hbm] * 3,
            out_specs=(hbm,) * 3,
            scratch_shapes=[
                *(pltpu.VMEM(shape.shape, shape.dtype) for shape in shapes),
                dma((pieces + 2,)), dma((pieces + 2,)),
            ],
            compiler_params=pltpu.CompilerParams(vmem_limit_bytes=62 << 20),
        )(new, rel, peak)
        return new.T, rel.reshape(total), peak.reshape(())

    spread = P(("rows", "grp"))
    return jax.shard_map(
        on_device,
        mesh=mesh,
        in_specs=(P(("rows", "grp"), None), P(("rows", "grp"), None), spread, spread, spread, P()),
        out_specs=(P(("rows", "grp"), None), spread, P()),
        check_vma=False,
    )
```
